1024 devices in a mesh: ctx: 64 (over x, y, z_hi), tp: 16 (over z_lo, core).
Axes of the slice: x: 4, y: 8, z: 16 (z_hi: 2, z_lo: 8; z = z_hi * 8 + z_lo), core: 2. Of those that a mesh axis runs over, the one named last changes fastest.
Arguments:
- streams: bfloat16 [3, 4096, 8192], P(None, 'tp', 'ctx'), may hold values from -6 to 6
- medium_taps: float32 [4096, 128], P('tp'), may hold values from -0.5 to 0.5
- decay_rates: float32 [4096, 16], P('tp'), may hold values from 5e-06 to 0.1
- mode_weights: float32 [4096, 16], P('tp'), may hold values from -1.5 to 1.5
- skip_gain: float32 [4096], P('tp'), may hold values from -1 to 1
Outputs:
- gated_output: bfloat16 [4096, 8192], P('tp', 'ctx')
The draws below stay inside these ranges and needn't reach their ends.
All inputs are finite; a program needn't handle non-finite values.
Results may differ from the reference program's by a relative error of at most 0.01.
Values may be sent and summed in bfloat16 or wider, within the bound.
A program may use at most 32 MiB of HBM per device.

```python
import math
import jax
import jax.numpy as jnp
from jax import lax

D = 4096
TAPS = 128
MODES = 16
TOKENS = 8192


def draw_decay_rates(key, part):
    first, second = jax.random.split(jax.random.fold_in(key, 7))
    lower, upper = (math.log(1e-05), math.log(0.05))
    base = jnp.exp(jax.random.uniform(first, (D, 1), jnp.float32, lower, upper))
    jitter = jax.random.uniform(second, (D, MODES), jnp.float32, 0.5, 2.0)
    return (base * jitter).astype(jnp.float32)


def block_levels(stream_key, dims, cuts, least, top_value):
    def one(dim, blocks):
        draws = jax.random.uniform(jax.random.fold_in(jax.random.fold_in(stream_key, 6), dim), (blocks,), jnp.float32, least / len(cuts), top_value / len(cuts))
        return jnp.repeat(jnp.exp(draws), dims[dim] // blocks).reshape((-1,) + (1,) * (len(dims) - dim - 1))

    level = one(*cuts[0])
    for cut in cuts[1:]:
        level = level * one(*cut)
    return level


def noise(rng, dims, scale, limit, cuts=(), dtype=jnp.bfloat16):
    values = jax.random.normal(rng, dims, jnp.float32) * scale
    if len(cuts) > 0:
        values = block_levels(rng, dims, cuts, -0.22, 0.18) * values
    return jnp.clip(values, min=-limit, max=limit).astype(dtype)


def setup_inputs(seed: int = 0) -> dict:
    streams_of = jax.random.split(jax.random.key(seed), 6)
    return {
        "streams": noise(streams_of[0], (3, D, TOKENS), 1.0, 6.0, ((1, 16), (2, 64))),
        "medium_taps": noise(streams_of[1], (D, TAPS), TAPS ** -0.5, 0.5, ((0, 16),), jnp.float32),
        "decay_rates": draw_decay_rates(jax.random.fold_in(streams_of[5], 71), 0),
        "mode_weights": noise(streams_of[3], (D, MODES), MODES ** -0.5, 1.5, ((0, 16),), jnp.float32),
        "skip_gain": jnp.clip(jax.random.uniform(streams_of[4], (D,), jnp.float32, -1.0, 1.0) * block_levels(streams_of[4], (D,), ((0, 16),), -0.4, 0.0), -1.0, 1.0),
    }


def causal_taps(padded, taps):
    kernel = jnp.flip(taps, 1)[:, None, :]
    result = lax.conv_general_dilated(padded[None], kernel, (1,), 'VALID', dimension_numbers=('NCH', 'OIH', 'NCH'), feature_group_count=taps.shape[0], precision=lax.Precision.HIGHEST)
    return result[0]

def modal_filter(rates, weights, length):
    times = jnp.arange(length).astype(jnp.float32)
    decay = jnp.exp(-rates[:, :, None] * times)
    scaled = weights * jnp.sqrt(2.0 * rates)
    return jnp.einsum('cr,crt->ct', scaled, decay, precision=lax.Precision.HIGHEST)

def reference(streams, medium_taps, decay_rates, mode_weights, skip_gain):
    width = 64
    count = D // width
    grouped = jnp.moveaxis(streams.reshape(3, count, width, TOKENS), 1, 0)
    blocks = (grouped, medium_taps.reshape(count, width, TAPS), decay_rates.reshape(count, width, MODES), mode_weights.reshape(count, width, MODES), skip_gain.reshape(count, width))

    def one_block(inputs):
        series, taps, rates, weights, direct = inputs
        padded = jnp.pad(series[2].astype(jnp.float32), ((0, 0), (TAPS - 1, 0)))
        medium = causal_taps(padded, taps)
        gated = lax.optimization_barrier((series[1].astype(jnp.float32) * medium).astype(jnp.bfloat16))
        signal = gated.astype(jnp.float32)
        filt = modal_filter(rates, weights, TOKENS)
        size = 2 * TOKENS
        spectrum = jnp.fft.rfft(signal, n=size) * jnp.fft.rfft(filt, n=size)
        whole_part = jnp.fft.irfft(spectrum, n=size)[:, :TOKENS]
        mixed = lax.optimization_barrier((whole_part + direct[:, None] * signal).astype(jnp.bfloat16))
        return (series[0].astype(jnp.float32) * mixed.astype(jnp.float32)).astype(jnp.bfloat16)
    return lax.map(one_block, blocks).reshape(D, TOKENS)
```

```python
import functools

import jax
import jax.numpy as jnp
from jax import lax
from jax.experimental import pallas as pl
from jax.experimental.pallas import tpu as pltpu
from jax.sharding import PartitionSpec as P

MESH = pl.DeviceIdType.MESH
F32 = jnp.float32
BF16 = jnp.bfloat16
X, Y, Z = 4, 8, 16
LANES = 128
CHUNK = 128
TAPS = 128
MODES = 16
SUBS = 8
STEP = CHUNK // SUBS
GROUPS = 2


def place():
    ctx = lax.axis_index("ctx")
    return ctx, lax.axis_index("tp"), ctx // 16, (ctx // 2) % 8, ctx % 2


def ctx_of(x, y, hi):
    return (lax.rem(x + X, X) * Y + lax.rem(y + Y, Y)) * 2 + hi


def kernel(
    streams, taps, rates, weights, skip, out,
    vbuf, kbuf, qbuf, traw, rraw, wraw, sraw, halo,
    xw, kw, tapsT, coef, rows, gated, local, carry, mixed,
    ybuf, xbuf, zbuf, in_sem, send_sem, halo_sem, y_sem, x_sem, z_sem,
):
    ctx, tp, x, y, hi = place()
    count = lax.axis_size("ctx")
    loads = []
    for n, (src, dst) in enumerate(
        ((rates, rraw), (weights, wraw), (taps, traw), (streams.at[2], vbuf),
         (streams.at[1], kbuf), (skip, sraw), (streams.at[0], qbuf))
    ):
        copy = pltpu.make_async_copy(src, dst, in_sem.at[n])
        copy.start()
        loads.append(copy)

    after = lax.rem(ctx + 1, count)
    before = lax.rem(ctx + count - 1, count)
    mate = ctx + 1 - 2 * hi
    partners = [after, before]
    partners += [ctx_of(x, y + d, hi) for d in range(1, Y)]
    partners += [ctx_of(x + d, y, hi) for d in range(1, X)]
    barrier = pltpu.get_barrier_semaphore()
    for p in partners:
        pl.semaphore_signal(barrier, inc=1, device_id=(p, tp), device_id_type=MESH)

    loads[0].wait()
    loads[1].wait()
    sub = lax.broadcasted_iota(jnp.int32, (SUBS, LANES), 0)
    subf = sub.astype(F32)
    yf = y.astype(F32)
    for g in range(GROUPS):
        part = pl.ds(g * LANES, LANES)
        rate = rraw[part, :].T
        weight = wraw[part, :].T
        rows[g, 0] = jnp.exp(-rate)
        rows[g, 1] = weight * jnp.sqrt(2.0 * rate)
        rows[g, 2] = jnp.exp(-128.0 * rate)
        rows[g, 3] = jnp.exp(-256.0 * rate)
        rows[g, 4] = jnp.exp(-2048.0 * rate)
        rows[g, 5] = jnp.exp((-256.0 * yf) * rate)
        rows[g, 6] = rate
        for r in range(MODES):
            lam = jnp.broadcast_to(rows[g, 6, r : r + 1, :], (SUBS, LANES))
            coef[g, r, 0] = jnp.where(sub >= 1, jnp.exp(-16.0 * lam), 0.0)
            coef[g, r, 1] = jnp.where(sub >= 2, jnp.exp(-32.0 * lam), 0.0)
            coef[g, r, 2] = jnp.where(sub >= 4, jnp.exp(-64.0 * lam), 0.0)
            coef[g, r, 3] = jnp.exp(-16.0 * subf * lam)

    pl.semaphore_wait(barrier, len(partners))
    sends = []
    for g in range(GROUPS):
        copy = pltpu.make_async_remote_copy(
            src_ref=streams.at[2, pl.ds(g * LANES, LANES), :],
            dst_ref=halo.at[g],
            send_sem=send_sem.at[g],
            recv_sem=halo_sem.at[g],
            device_id=(after, tp),
            device_id_type=MESH,
        )
        copy.start()
        sends.append(copy)

    loads[2].wait()
    loads[3].wait()
    loads[4].wait()
    loads[5].wait()
    for g in range(GROUPS):
        part = pl.ds(g * LANES, LANES)
        tapsT[g] = traw[part, :].T
        xw[g, pl.ds(CHUNK, CHUNK), :] = vbuf[part, :].astype(F32).T
        kw[g] = kbuf[part, :].astype(F32).T

    def exchange(g, which, src, dst_of, sem, devices):
        for n, d in enumerate(devices):
            copy = pltpu.make_async_remote_copy(
                src_ref=src,
                dst_ref=dst_of(n),
                send_sem=send_sem.at[2 + g * 11 + which + n],
                recv_sem=sem.at[g, n],
                device_id=(d, tp),
                device_id_type=MESH,
            )
            copy.start()
            sends.append(copy)
            yield copy

    y_copies, x_copies, z_copies = {}, {}, {}
    for g in range(GROUPS):
        sends[g].wait_recv()
        past = halo[g].astype(F32).T
        xw[g, pl.ds(0, CHUNK), :] = jnp.where(ctx > 0, past, 0.0)

        def fir(block, acc):
            base = CHUNK - 8 * block
            tap = [
                jnp.broadcast_to(tapsT[g, pl.ds(8 * block + jj, 1), :], (SUBS, LANES))
                for jj in range(8)
            ]
            window = {
                m: xw[g, pl.ds(base + m, SUBS, stride=STEP), :] for m in range(-7, STEP)
            }
            acc = list(acc)
            for jj in range(8):
                for i in range(STEP):
                    acc[i] = acc[i] + tap[jj] * window[i - jj]
            return tuple(acc)

        zero = jnp.zeros((SUBS, LANES), F32)
        medium = lax.fori_loop(0, TAPS // 8, fir, (zero,) * STEP)
        gate = []
        for i in range(STEP):
            key = kw[g, pl.ds(i, SUBS, stride=STEP), :]
            value = (key * medium[i]).astype(BF16).astype(F32)
            gated[g, i] = value
            gate.append(value)
        for r in range(MODES):
            a = jnp.broadcast_to(rows[g, 0, r : r + 1, :], (SUBS, LANES))
            h = gate[0]
            for i in range(1, STEP):
                h = h * a + gate[i]
            h = h + coef[g, r, 0] * pltpu.roll(h, 1, 0)
            h = h + coef[g, r, 1] * pltpu.roll(h, 2, 0)
            h = h + coef[g, r, 2] * pltpu.roll(h, 4, 0)
            carry[g, r] = jnp.where(sub >= 1, pltpu.roll(h, 1, 0), 0.0)
            ybuf[g, 0, pl.ds(r, 1), :] = h[SUBS - 1 : SUBS, :]
        y_copies[g] = list(
            exchange(
                g, 0, ybuf.at[g, 0], lambda n, g=g: ybuf.at[g, n + 1], y_sem,
                [ctx_of(x, y + d, hi) for d in range(1, Y)],
            )
        )

    for g in range(GROUPS):
        direct = jnp.broadcast_to(sraw[g : g + 1, :], (SUBS, LANES))
        start = tuple(direct * gated[g, i] for i in range(STEP))

        def modes(block, acc):
            acc = list(acc)
            for rr in range(4):
                r = 4 * block + rr
                a = jnp.broadcast_to(rows[g, 0, pl.ds(r, 1), :], (SUBS, LANES))
                w = jnp.broadcast_to(rows[g, 1, pl.ds(r, 1), :], (SUBS, LANES))
                h = a * carry[g, r] + gated[g, 0]
                acc[0] = acc[0] + w * h
                for i in range(1, STEP):
                    h = h * a + gated[g, i]
                    acc[i] = acc[i] + w * h
            return tuple(acc)

        total = lax.fori_loop(0, MODES // 4, modes, start)
        for i in range(STEP):
            local[g, i] = total[i]

    before_rows = {}
    for g in range(GROUPS):
        for copy in y_copies[g]:
            copy.wait_recv()
        two = rows[g, 3]
        prefix = jnp.zeros((MODES, LANES), F32)
        total = jnp.zeros((MODES, LANES), F32)
        for yy in range(Y):
            part = ybuf[g, lax.rem(y - yy + Y, Y)]
            total = total * two + part
            prefix = jnp.where(yy < y, prefix * two + part, prefix)
        before_rows[g] = prefix
        xbuf[g, 0] = total
        x_copies[g] = list(
            exchange(
                g, 7, xbuf.at[g, 0], lambda n, g=g: xbuf.at[g, n + 1], x_sem,
                [ctx_of(x + d, y, hi) for d in range(1, X)],
            )
        )
    own = {}
    for g in range(GROUPS):
        for copy in x_copies[g]:
            copy.wait_recv()
        acc = jnp.zeros((MODES, LANES), F32)
        for xx in range(X):
            part = xbuf[g, lax.rem(x - xx + X, X)]
            acc = jnp.where(xx < x, acc * rows[g, 4] + part, acc)
        plane = before_rows[g] + rows[g, 5] * acc
        one, two = rows[g, 2], rows[g, 3]
        own[g] = one * plane
        zbuf[g, 0] = jnp.where(hi == 0, two * plane + ybuf[g, 0], plane)
        z_copies[g] = list(
            exchange(g, 10, zbuf.at[g, 0], lambda n, g=g: zbuf.at[g, 1], z_sem, [mate])
        )
    loads[6].wait()
    for g in range(GROUPS):
        z_copies[g][0].wait_recv()
        rows[g, 6] = own[g] + zbuf[g, 1]
        acc = [local[g, i] for i in range(STEP)]
        for r in range(MODES):
            a = jnp.broadcast_to(rows[g, 0, r : r + 1, :], (SUBS, LANES))
            w = jnp.broadcast_to(rows[g, 1, r : r + 1, :], (SUBS, LANES))
            state = jnp.broadcast_to(rows[g, 6, r : r + 1, :], (SUBS, LANES))
            q = (w * a) * (coef[g, r, 3] * state)
            acc[0] = acc[0] + q
            for i in range(1, STEP):
                q = q * a
                acc[i] = acc[i] + q
        for i in range(STEP):
            mixed[g, pl.ds(i, SUBS, stride=STEP), :] = acc[i]
        part = pl.ds(g * LANES, LANES)
        back = mixed[g].T.astype(BF16).astype(F32)
        out[part, :] = (qbuf[part, :].astype(F32) * back).astype(BF16)
    for copy in sends:
        copy.wait_send()


def local(streams, medium_taps, decay_rates, mode_weights, skip_gain):
    channels = streams.shape[1]
    anywhere = pl.BlockSpec(memory_space=pltpu.MemorySpace.HBM)
    vmem = pltpu.VMEM
    dma = pltpu.SemaphoreType.DMA
    return pl.pallas_call(
        kernel,
        out_shape=jax.ShapeDtypeStruct((channels, CHUNK), BF16),
        in_specs=[anywhere] * 5,
        out_specs=pl.BlockSpec(memory_space=pltpu.VMEM),
        scratch_shapes=[
            vmem((channels, CHUNK), BF16),
            vmem((channels, CHUNK), BF16),
            vmem((channels, CHUNK), BF16),
            vmem((channels, TAPS), F32),
            vmem((channels, MODES), F32),
            vmem((channels, MODES), F32),
            vmem((GROUPS, LANES), F32),
            vmem((GROUPS, LANES, CHUNK), BF16),
            vmem((GROUPS, 2 * CHUNK, LANES), F32),
            vmem((GROUPS, CHUNK, LANES), F32),
            vmem((GROUPS, TAPS, LANES), F32),
            vmem((GROUPS, MODES, 4, SUBS, LANES), F32),
            vmem((GROUPS, 7, MODES, LANES), F32),
            vmem((GROUPS, STEP, SUBS, LANES), F32),
            vmem((GROUPS, STEP, SUBS, LANES), F32),
            vmem((GROUPS, MODES, SUBS, LANES), F32),
            vmem((GROUPS, CHUNK, LANES), F32),
            vmem((GROUPS, Y, MODES, LANES), F32),
            vmem((GROUPS, X, MODES, LANES), F32),
            vmem((GROUPS, 2, MODES, LANES), F32),
            dma((7,)),
            dma((2 + GROUPS * 11,)),
            dma((GROUPS,)),
            dma((GROUPS, Y - 1)),
            dma((GROUPS, X - 1)),
            dma((GROUPS, 1)),
        ],
        name="gated_modal",
        compiler_params=pltpu.CompilerParams(collective_id=0, has_side_effects=True),
    )(streams, medium_taps, decay_rates, mode_weights, skip_gain.reshape(GROUPS, LANES))


def solution(mesh):
    placed = (P(None, "tp", "ctx"), P("tp", None), P("tp", None), P("tp", None), P("tp"))
    return jax.shard_map(
        local, mesh=mesh, in_specs=placed, out_specs=P("tp", "ctx"), check_vma=False
    )
```

```python
import jax
import jax.numpy as jnp
from jax import lax
from jax.experimental import pallas as pl
from jax.experimental.pallas import tpu as pltpu
from jax.sharding import PartitionSpec as P

MESH = pl.DeviceIdType.MESH
F32 = jnp.float32
BF16 = jnp.bfloat16
X, Y = 4, 8
LANES = 128
CHUNK = 128
TAPS = 128
MODES = 16
SUBS = 8
STEP = CHUNK // SUBS
TILES = CHUNK // SUBS
GROUPS = 2
EVEN, ODD, PAST = 0, 1, 2


def ctx_of(x, y, hi):
    return (lax.rem(x + X, X) * Y + lax.rem(y + Y, Y)) * 2 + hi


def remote(src, dst, send, recv, ctx):
    return pltpu.make_async_remote_copy(
        src_ref=src,
        dst_ref=dst,
        send_sem=send,
        recv_sem=recv,
        device_id=(ctx, lax.axis_index("tp")),
        device_id_type=MESH,
    )


def wide(row):
    return jnp.broadcast_to(row, (SUBS, LANES))


def kernel(
    streams, taps, rates, weights, skip, out,
    vbuf, kbuf, qbuf, traw, rates_t, weights_t, direct,
    raw, past, tokens, keys, medium, series, coef, rows, gated, local, carry, mixed,
    state, ybuf, xbuf, zbuf,
    in_sem, raw_send, raw_sem, past_send, past_sem, back_send,
    y_send, y_sem, x_send, x_sem, z_send, z_sem,
):
    ctx = lax.axis_index("ctx")
    tp = lax.axis_index("tp")
    x, y, hi = ctx // 16, (ctx // 2) % 8, ctx % 2
    mate = ctx + 1 - 2 * hi
    count = lax.axis_size("ctx")
    following = lax.rem(ctx + 2, count)
    previous = lax.rem(ctx + count - 2, count)
    row_devices = [ctx_of(x, y + d, hi) for d in range(1, Y)]
    column_devices = [ctx_of(x + d, y, hi) for d in range(1, X)]
    barrier = pltpu.get_barrier_semaphore()
    part = [pl.ds(g * LANES, LANES) for g in range(GROUPS)]

    def raw_copy(which, g):
        return remote(
            streams.at[2 - which, part[g], :], raw.at[which, g],
            raw_send.at[which, g], raw_sem.at[which, g], mate,
        )

    def forward_copy(g):
        return remote(raw.at[0, g], past.at[g], past_send.at[g], past_sem.at[g], following)

    def back_copy(g):
        return remote(streams.at[2, part[g], :], past.at[g], back_send.at[g], past_sem.at[g], mate)

    def y_copy(g, n):
        return remote(
            ybuf.at[g, 0], ybuf.at[g, n + 1], y_send.at[g, n], y_sem.at[g, n], row_devices[n]
        )

    def x_copy(g, n):
        return remote(
            xbuf.at[g, 0], xbuf.at[g, n + 1], x_send.at[g, n], x_sem.at[g, n], column_devices[n]
        )

    def z_copy(g):
        return remote(zbuf.at[g, 0], zbuf.at[g, 1], z_send.at[g], z_sem.at[g], mate)

    @pl.when(hi == 0)
    def _():
        pl.semaphore_signal(barrier, inc=1, device_id=(mate, tp), device_id_type=MESH)
        for p in [following, previous] + row_devices + column_devices:
            pl.semaphore_signal(barrier, inc=1, device_id=(p, tp), device_id_type=MESH)

    @pl.when(hi == 1)
    def _():
        pl.semaphore_wait(barrier, 1)
        for which in range(2):
            for g in range(GROUPS):
                raw_copy(which, g).start()

    loads = []
    for n, (src, dst) in enumerate(
        ((rates, rates_t), (weights, weights_t), (taps, traw), (streams.at[2], vbuf),
         (streams.at[1], kbuf), (skip, direct), (streams.at[0], qbuf))
    ):
        copy = pltpu.make_async_copy(src, dst, in_sem.at[n])
        copy.start()
        loads.append(copy)

    sub = lax.broadcasted_iota(jnp.int32, (SUBS, LANES), 0)
    subf = sub.astype(F32)
    yf = y.astype(F32)
    loads[0].wait()
    loads[1].wait()
    for g in range(GROUPS):
        rate = rates_t[:, part[g]]
        rows[g, 0] = jnp.exp(-rate)
        rows[g, 1] = weights_t[:, part[g]] * jnp.sqrt(2.0 * rate)
        rows[g, 2] = jnp.exp(-128.0 * rate)
        rows[g, 3] = jnp.exp(-256.0 * rate)
        rows[g, 4] = jnp.exp(-2048.0 * rate)
        rows[g, 5] = jnp.exp((-256.0 * yf) * rate)
        for r in range(MODES):
            lam = wide(rates_t[r : r + 1, part[g]])
            coef[g, r, 0] = jnp.where(sub >= 1, jnp.exp(-16.0 * lam), 0.0)
            coef[g, r, 1] = jnp.where(sub >= 2, jnp.exp(-32.0 * lam), 0.0)
            coef[g, r, 2] = jnp.where(sub >= 4, jnp.exp(-64.0 * lam), 0.0)
            coef[g, r, 3] = jnp.exp(-16.0 * subf * lam)
    for n in range(2, 7):
        loads[n].wait()
    zeros = jnp.zeros((SUBS, LANES), F32)

    def lay(which, g, block):
        tokens[which, g, pl.ds(0, SUBS), :] = zeros
        tokens[which, g, pl.ds(SUBS, CHUNK), :] = block.astype(F32).T
        tokens[which, g, pl.ds(SUBS + CHUNK, SUBS), :] = zeros

    for g in range(GROUPS):
        traw[part[g], :] = traw[part[g], :].T

    def within(which, g, acc):
        def body(b, acc):
            acc = list(acc)
            window = [
                tokens[which, g, pl.ds(SUBS + SUBS * q - b, SUBS), :] for q in range(TILES)
            ]
            for a in range(TILES):
                tap = wide(traw[pl.ds(g * TAPS + SUBS * a + b, 1), :])
                for p in range(a, TILES):
                    acc[p] = acc[p] + tap * window[p - a]
            return tuple(acc)

        return lax.fori_loop(0, SUBS, body, tuple(acc))

    def across(which, g, acc):
        def body(b, acc):
            acc = list(acc)
            window = [
                tokens[which, g, pl.ds(2 * SUBS + SUBS * q - b, SUBS), :] for q in range(TILES)
            ]
            for a in range(TILES):
                tap = wide(traw[pl.ds(g * TAPS + SUBS * a + b, 1), :])
                for p in range(a + 1):
                    acc[p] = acc[p] + tap * window[TILES - 1 + p - a]
            return tuple(acc)

        return lax.fori_loop(0, SUBS, body, tuple(acc))

    def keep(which, g, acc):
        for p in range(TILES):
            medium[which, g, p] = acc[p]

    def kept(which, g):
        return tuple(medium[which, g, p] for p in range(TILES))

    def ends(which, g, acc, mine):
        for p in range(TILES):
            key = keys[which, g, pl.ds(SUBS * p, SUBS), :]
            series[which, g, pl.ds(SUBS * p, SUBS), :] = (key * acc[p]).astype(BF16).astype(F32)
        gate = [series[which, g, pl.ds(i, SUBS, stride=STEP), :] for i in range(STEP)]
        if mine:
            for i in range(STEP):
                gated[g, i] = gate[i]
        for r in range(MODES):
            a = wide(rows[g, 0, r : r + 1, :])
            h = gate[0]
            for i in range(1, STEP):
                h = h * a + gate[i]
            h = h + coef[g, r, 0] * pltpu.roll(h, 1, 0)
            h = h + coef[g, r, 1] * pltpu.roll(h, 2, 0)
            h = h + coef[g, r, 2] * pltpu.roll(h, 4, 0)
            if mine:
                carry[g, r] = jnp.where(sub >= 1, pltpu.roll(h, 1, 0), 0.0)
            state[which, g, pl.ds(r, 1), :] = h[SUBS - 1 : SUBS, :]

    def respond(g):
        skipped = wide(direct[g : g + 1, :])
        start = tuple(skipped * gated[g, i] for i in range(STEP))

        def modes(block, acc):
            acc = list(acc)
            for rr in range(4):
                r = 4 * block + rr
                a = wide(rows[g, 0, pl.ds(r, 1), :])
                w = wide(rows[g, 1, pl.ds(r, 1), :])
                h = a * carry[g, r] + gated[g, 0]
                acc[0] = acc[0] + w * h
                for i in range(1, STEP):
                    h = h * a + gated[g, i]
                    acc[i] = acc[i] + w * h
            return tuple(acc)

        total = lax.fori_loop(0, MODES // 4, modes, start)
        for i in range(STEP):
            local[g, i] = total[i]

    def finish(g, held, n):
        acc = [local[g, i] for i in range(STEP)]
        for r in range(MODES):
            a = wide(rows[g, 0, r : r + 1, :])
            w = wide(rows[g, 1, r : r + 1, :])
            q = (w * a) * (coef[g, r, 3] * wide(held[g, n, r : r + 1, :]))
            acc[0] = acc[0] + q
            for i in range(1, STEP):
                q = q * a
                acc[i] = acc[i] + q
        for i in range(STEP):
            mixed[g, pl.ds(i, SUBS, stride=STEP), :] = acc[i]
        back = mixed[g].T.astype(BF16).astype(F32)
        out[part[g], :] = (qbuf[part[g], :].astype(F32) * back).astype(BF16)

    @pl.when(hi == 0)
    def _():
        for g in range(GROUPS):
            lay(EVEN, g, vbuf[part[g], :])
            keys[EVEN, g] = kbuf[part[g], :].astype(F32).T
            keep(EVEN, g, within(EVEN, g, (zeros,) * TILES))
            keep(ODD, g, across(EVEN, g, (zeros,) * TILES))
        pl.semaphore_wait(barrier, Y + X)
        for g in range(GROUPS):
            raw_copy(0, g).wait_recv()
            forward_copy(g).start()
        for g in range(GROUPS):
            back_copy(g).start()
        for g in range(GROUPS):
            lay(ODD, g, raw[0, g])
            keep(ODD, g, within(ODD, g, kept(ODD, g)))
        for g in range(GROUPS):
            raw_copy(1, g).wait_recv()
            keys[ODD, g] = raw[1, g].astype(F32).T
            ends(ODD, g, kept(ODD, g), False)
        for g in range(GROUPS):
            forward_copy(g).wait_recv()
            lay(PAST, g, jnp.where(ctx > 0, past[g].astype(F32), 0.0))
            ends(EVEN, g, across(PAST, g, kept(EVEN, g)), True)
            ybuf[g, 0] = rows[g, 2] * state[EVEN, g] + state[ODD, g]
            for n in range(Y - 1):
                y_copy(g, n).start()
        for g in range(GROUPS):
            respond(g)
        prefixes = []
        for g in range(GROUPS):
            for n in range(Y - 1):
                y_copy(g, n).wait_recv()
            two = rows[g, 3]
            prefix = jnp.zeros((MODES, LANES), F32)
            total = jnp.zeros((MODES, LANES), F32)
            for yy in range(Y):
                term = ybuf[g, lax.rem(y - yy + Y, Y)]
                total = total * two + term
                prefix = jnp.where(yy < y, prefix * two + term, prefix)
            prefixes.append(prefix)
            xbuf[g, 0] = total
            for n in range(X - 1):
                x_copy(g, n).start()
        for g in range(GROUPS):
            for n in range(X - 1):
                x_copy(g, n).wait_recv()
            acc = jnp.zeros((MODES, LANES), F32)
            for xx in range(X):
                term = xbuf[g, lax.rem(x - xx + X, X)]
                acc = jnp.where(xx < x, acc * rows[g, 4] + term, acc)
            plane = prefixes[g] + rows[g, 5] * acc
            zbuf[g, 1] = plane
            zbuf[g, 0] = rows[g, 2] * plane + state[EVEN, g]
            z_copy(g).start()
        for g in range(GROUPS):
            finish(g, zbuf, 1)
        for g in range(GROUPS):
            forward_copy(g).wait_send()
            back_copy(g).wait_send()
            for n in range(Y - 1):
                y_copy(g, n).wait_send()
            for n in range(X - 1):
                x_copy(g, n).wait_send()
            z_copy(g).wait_send()

    @pl.when(hi == 1)
    def _():
        for g in range(GROUPS):
            lay(ODD, g, vbuf[part[g], :])
            keys[ODD, g] = kbuf[part[g], :].astype(F32).T
            keep(ODD, g, within(ODD, g, (zeros,) * TILES))
        for g in range(GROUPS):
            back_copy(g).wait_recv()
            lay(EVEN, g, past[g])
            ends(ODD, g, across(EVEN, g, kept(ODD, g)), True)
            respond(g)
        for g in range(GROUPS):
            z_copy(g).wait_recv()
            finish(g, zbuf, 1)
        for which in range(2):
            for g in range(GROUPS):
                raw_copy(which, g).wait_send()


def local(streams, medium_taps, decay_rates, mode_weights, skip_gain):
    channels = streams.shape[1]
    hbm = pl.BlockSpec(memory_space=pltpu.MemorySpace.HBM)
    vmem = pltpu.VMEM
    dma = pltpu.SemaphoreType.DMA
    return pl.pallas_call(
        kernel,
        out_shape=jax.ShapeDtypeStruct((channels, CHUNK), BF16),
        in_specs=[hbm] * 5,
        out_specs=pl.BlockSpec(memory_space=pltpu.VMEM),
        scratch_shapes=[
            vmem((channels, CHUNK), BF16),
            vmem((channels, CHUNK), BF16),
            vmem((channels, CHUNK), BF16),
            vmem((channels, TAPS), F32),
            vmem((MODES, channels), F32),
            vmem((MODES, channels), F32),
            vmem((GROUPS, LANES), F32),
            vmem((2, GROUPS, LANES, CHUNK), BF16),
            vmem((GROUPS, LANES, CHUNK), BF16),
            vmem((3, GROUPS, CHUNK + 2 * SUBS, LANES), F32),
            vmem((2, GROUPS, CHUNK, LANES), F32),
            vmem((2, GROUPS, TILES, SUBS, LANES), F32),
            vmem((2, GROUPS, CHUNK, LANES), F32),
            vmem((GROUPS, MODES, 4, SUBS, LANES), F32),
            vmem((GROUPS, 6, MODES, LANES), F32),
            vmem((GROUPS, STEP, SUBS, LANES), F32),
            vmem((GROUPS, STEP, SUBS, LANES), F32),
            vmem((GROUPS, MODES, SUBS, LANES), F32),
            vmem((GROUPS, CHUNK, LANES), F32),
            vmem((2, GROUPS, MODES, LANES), F32),
            vmem((GROUPS, Y, MODES, LANES), F32),
            vmem((GROUPS, X, MODES, LANES), F32),
            vmem((GROUPS, 2, MODES, LANES), F32),
            dma((7,)),
            dma((2, GROUPS)),
            dma((2, GROUPS)),
            dma((GROUPS,)),
            dma((GROUPS,)),
            dma((GROUPS,)),
            dma((GROUPS, Y - 1)),
            dma((GROUPS, Y - 1)),
            dma((GROUPS, X - 1)),
            dma((GROUPS, X - 1)),
            dma((GROUPS,)),
            dma((GROUPS,)),
        ],
        name="gated_modal",
        compiler_params=pltpu.CompilerParams(collective_id=0, has_side_effects=True),
    )(
        streams,
        medium_taps,
        decay_rates.T,
        mode_weights.T,
        skip_gain.reshape(GROUPS, LANES),
    )


def solution(mesh):
    placed = (P(None, "tp", "ctx"), P("tp", None), P("tp", None), P("tp", None), P("tp"))
    return jax.shard_map(
        local, mesh=mesh, in_specs=placed, out_specs=P("tp", "ctx"), check_vma=False
    )
```

```python
import jax
import jax.numpy as jnp
from jax import lax
from jax.experimental import pallas as pl
from jax.experimental.pallas import tpu as pltpu
from jax.sharding import PartitionSpec as P

MESH = pl.DeviceIdType.MESH
F32 = jnp.float32
BF16 = jnp.bfloat16
X, Y = 4, 8
LANES = 128
CHUNK = 128
TAPS = 128
MODES = 16
SUBS = 8
STEP = CHUNK // SUBS
TILES = CHUNK // SUBS
GROUPS = 2
EVEN, ODD, PAST = 0, 1, 2


def ctx_of(x, y, hi):
    return (lax.rem(x + X, X) * Y + lax.rem(y + Y, Y)) * 2 + hi


def remote(src, dst, send, recv, ctx):
    return pltpu.make_async_remote_copy(
        src_ref=src,
        dst_ref=dst,
        send_sem=send,
        recv_sem=recv,
        device_id=(ctx, lax.axis_index("tp")),
        device_id_type=MESH,
    )


def wide(row):
    return jnp.broadcast_to(row, (SUBS, LANES))


def kernel(
    streams, taps, rates, weights, skip, out,
    vbuf, kbuf, qbuf, traw, rates_t, weights_t, direct,
    raw, past, tokens, keys, medium, series, coef, rows, gated, local, carry, mixed,
    state, ybuf, xbuf, zbuf,
    in_sem, raw_send, raw_sem, past_send, past_sem, back_send,
    y_send, y_sem, x_send, x_sem, z_send, z_sem,
):
    ctx = lax.axis_index("ctx")
    tp = lax.axis_index("tp")
    x, y, hi = ctx // 16, (ctx // 2) % 8, ctx % 2
    low = tp // 2
    later = jnp.logical_or(low == 5, low == 7)
    mate = ctx + 1 - 2 * hi
    count = lax.axis_size("ctx")
    following = lax.rem(ctx + 2, count)
    previous = lax.rem(ctx + count - 2, count)
    row_devices = [ctx_of(x, y + d, hi) for d in range(1, Y)]
    column_devices = [ctx_of(x + d, y, hi) for d in range(1, X)]
    barrier = pltpu.get_barrier_semaphore()
    part = [pl.ds(g * LANES, LANES) for g in range(GROUPS)]

    def raw_copy(which, g):
        return remote(
            streams.at[2 - which, part[g], :], raw.at[which, g],
            raw_send.at[which, g], raw_sem.at[which, g], mate,
        )

    def forward_copy(g):
        return remote(raw.at[0, g], past.at[g], past_send.at[g], past_sem.at[g], following)

    def back_copy(g):
        return remote(streams.at[2, part[g], :], past.at[g], back_send.at[g], past_sem.at[g], mate)

    def y_copy(g, n):
        return remote(
            ybuf.at[g, 0], ybuf.at[g, n + 1], y_send.at[g, n], y_sem.at[g, n], row_devices[n]
        )

    def x_copy(g, n):
        return remote(
            xbuf.at[g, 0], xbuf.at[g, n + 1], x_send.at[g, n], x_sem.at[g, n], column_devices[n]
        )

    def z_copy(g):
        return remote(zbuf.at[g, 0], zbuf.at[g, 1], z_send.at[g], z_sem.at[g], mate)

    @pl.when(hi == 0)
    def _():
        pl.semaphore_signal(barrier, inc=1, device_id=(mate, tp), device_id_type=MESH)
        for p in [following, previous] + row_devices + column_devices:
            pl.semaphore_signal(barrier, inc=1, device_id=(p, tp), device_id_type=MESH)

    @pl.when(hi == 1)
    def _():
        pl.semaphore_wait(barrier, 1)

        @pl.when(jnp.logical_not(later))
        def _():
            for which in range(2):
                for g in range(GROUPS):
                    raw_copy(which, g).start()

    loads = []
    for n, (src, dst) in enumerate(
        ((rates, rates_t), (weights, weights_t), (taps, traw), (streams.at[2], vbuf),
         (streams.at[1], kbuf), (skip, direct), (streams.at[0], qbuf))
    ):
        copy = pltpu.make_async_copy(src, dst, in_sem.at[n])
        copy.start()
        loads.append(copy)

    sub = lax.broadcasted_iota(jnp.int32, (SUBS, LANES), 0)
    subf = sub.astype(F32)
    yf = y.astype(F32)
    loads[0].wait()
    loads[1].wait()
    for g in range(GROUPS):
        rate = rates_t[:, part[g]]
        rows[g, 0] = jnp.exp(-rate)
        rows[g, 1] = weights_t[:, part[g]] * jnp.sqrt(2.0 * rate)
        rows[g, 2] = jnp.exp(-128.0 * rate)
        rows[g, 3] = jnp.exp(-256.0 * rate)
        rows[g, 4] = jnp.exp(-2048.0 * rate)
        rows[g, 5] = jnp.exp((-256.0 * yf) * rate)
        for r in range(MODES):
            lam = wide(rates_t[r : r + 1, part[g]])
            coef[g, r, 0] = jnp.where(sub >= 1, jnp.exp(-16.0 * lam), 0.0)
            coef[g, r, 1] = jnp.where(sub >= 2, jnp.exp(-32.0 * lam), 0.0)
            coef[g, r, 2] = jnp.where(sub >= 4, jnp.exp(-64.0 * lam), 0.0)
            coef[g, r, 3] = jnp.exp(-16.0 * subf * lam)
    for n in range(2, 7):
        loads[n].wait()
    zeros = jnp.zeros((SUBS, LANES), F32)

    def lay(which, g, block):
        tokens[which, g, pl.ds(0, SUBS), :] = zeros
        tokens[which, g, pl.ds(SUBS, CHUNK), :] = block.astype(F32).T
        tokens[which, g, pl.ds(SUBS + CHUNK, SUBS), :] = zeros

    for g in range(GROUPS):
        traw[part[g], :] = traw[part[g], :].T

    def within(which, g, acc):
        def body(b, acc):
            acc = list(acc)
            window = [
                tokens[which, g, pl.ds(SUBS + SUBS * q - b, SUBS), :] for q in range(TILES)
            ]
            for a in range(TILES):
                tap = wide(traw[pl.ds(g * TAPS + SUBS * a + b, 1), :])
                for p in range(a, TILES):
                    acc[p] = acc[p] + tap * window[p - a]
            return tuple(acc)

        return lax.fori_loop(0, SUBS, body, tuple(acc))

    def across(which, g, acc):
        def body(b, acc):
            acc = list(acc)
            window = [
                tokens[which, g, pl.ds(2 * SUBS + SUBS * q - b, SUBS), :] for q in range(TILES)
            ]
            for a in range(TILES):
                tap = wide(traw[pl.ds(g * TAPS + SUBS * a + b, 1), :])
                for p in range(a + 1):
                    acc[p] = acc[p] + tap * window[TILES - 1 + p - a]
            return tuple(acc)

        return lax.fori_loop(0, SUBS, body, tuple(acc))

    def keep(which, g, acc):
        for p in range(TILES):
            medium[which, g, p] = acc[p]

    def kept(which, g):
        return tuple(medium[which, g, p] for p in range(TILES))

    def ends(which, g, acc, mine):
        for p in range(TILES):
            key = keys[which, g, pl.ds(SUBS * p, SUBS), :]
            series[which, g, pl.ds(SUBS * p, SUBS), :] = (key * acc[p]).astype(BF16).astype(F32)
        gate = [series[which, g, pl.ds(i, SUBS, stride=STEP), :] for i in range(STEP)]
        if mine:
            for i in range(STEP):
                gated[g, i] = gate[i]
        for r in range(MODES):
            a = wide(rows[g, 0, r : r + 1, :])
            h = gate[0]
            for i in range(1, STEP):
                h = h * a + gate[i]
            h = h + coef[g, r, 0] * pltpu.roll(h, 1, 0)
            h = h + coef[g, r, 1] * pltpu.roll(h, 2, 0)
            h = h + coef[g, r, 2] * pltpu.roll(h, 4, 0)
            if mine:
                carry[g, r] = jnp.where(sub >= 1, pltpu.roll(h, 1, 0), 0.0)
            state[which, g, pl.ds(r, 1), :] = h[SUBS - 1 : SUBS, :]

    def respond(g):
        skipped = wide(direct[g : g + 1, :])
        start = tuple(skipped * gated[g, i] for i in range(STEP))

        def modes(block, acc):
            acc = list(acc)
            for rr in range(4):
                r = 4 * block + rr
                a = wide(rows[g, 0, pl.ds(r, 1), :])
                w = wide(rows[g, 1, pl.ds(r, 1), :])
                h = a * carry[g, r] + gated[g, 0]
                acc[0] = acc[0] + w * h
                for i in range(1, STEP):
                    h = h * a + gated[g, i]
                    acc[i] = acc[i] + w * h
            return tuple(acc)

        total = lax.fori_loop(0, MODES // 4, modes, start)
        for i in range(STEP):
            local[g, i] = total[i]

    def finish(g, held, n):
        acc = [local[g, i] for i in range(STEP)]
        for r in range(MODES):
            a = wide(rows[g, 0, r : r + 1, :])
            w = wide(rows[g, 1, r : r + 1, :])
            q = (w * a) * (coef[g, r, 3] * wide(held[g, n, r : r + 1, :]))
            acc[0] = acc[0] + q
            for i in range(1, STEP):
                q = q * a
                acc[i] = acc[i] + q
        for i in range(STEP):
            mixed[g, pl.ds(i, SUBS, stride=STEP), :] = acc[i]
        back = mixed[g].T.astype(BF16).astype(F32)
        out[part[g], :] = (qbuf[part[g], :].astype(F32) * back).astype(BF16)

    @pl.when(hi == 0)
    def _():
        for g in range(GROUPS):
            lay(EVEN, g, vbuf[part[g], :])
            keys[EVEN, g] = kbuf[part[g], :].astype(F32).T
            keep(EVEN, g, within(EVEN, g, (zeros,) * TILES))
            keep(ODD, g, across(EVEN, g, (zeros,) * TILES))
        pl.semaphore_wait(barrier, Y + X)
        for g in range(GROUPS):
            raw_copy(0, g).wait_recv()
            forward_copy(g).start()
        for g in range(GROUPS):
            back_copy(g).start()
        for g in range(GROUPS):
            lay(ODD, g, raw[0, g])
            keep(ODD, g, within(ODD, g, kept(ODD, g)))
        for g in range(GROUPS):
            forward_copy(g).wait_recv()
            lay(PAST, g, jnp.where(ctx > 0, past[g].astype(F32), 0.0))
            ends(EVEN, g, across(PAST, g, kept(EVEN, g)), True)
        for g in range(GROUPS):
            raw_copy(1, g).wait_recv()
            keys[ODD, g] = raw[1, g].astype(F32).T
            ends(ODD, g, kept(ODD, g), False)
            ybuf[g, 0] = rows[g, 2] * state[EVEN, g] + state[ODD, g]
            for n in range(Y - 1):
                y_copy(g, n).start()
        for g in range(GROUPS):
            respond(g)
        prefixes = []
        for g in range(GROUPS):
            for n in range(Y - 1):
                y_copy(g, n).wait_recv()
            two = rows[g, 3]
            prefix = jnp.zeros((MODES, LANES), F32)
            total = jnp.zeros((MODES, LANES), F32)
            for yy in range(Y):
                term = ybuf[g, lax.rem(y - yy + Y, Y)]
                total = total * two + term
                prefix = jnp.where(yy < y, prefix * two + term, prefix)
            prefixes.append(prefix)
            xbuf[g, 0] = total
            for n in range(X - 1):
                x_copy(g, n).start()
        for g in range(GROUPS):
            for n in range(X - 1):
                x_copy(g, n).wait_recv()
            acc = jnp.zeros((MODES, LANES), F32)
            for xx in range(X):
                term = xbuf[g, lax.rem(x - xx + X, X)]
                acc = jnp.where(xx < x, acc * rows[g, 4] + term, acc)
            plane = prefixes[g] + rows[g, 5] * acc
            zbuf[g, 1] = plane
            zbuf[g, 0] = rows[g, 2] * plane + state[EVEN, g]
            z_copy(g).start()
        for g in range(GROUPS):
            finish(g, zbuf, 1)
        for g in range(GROUPS):
            forward_copy(g).wait_send()
            back_copy(g).wait_send()
            for n in range(Y - 1):
                y_copy(g, n).wait_send()
            for n in range(X - 1):
                x_copy(g, n).wait_send()
            z_copy(g).wait_send()

    @pl.when(hi == 1)
    def _():
        for g in range(GROUPS):
            lay(ODD, g, vbuf[part[g], :])
            keys[ODD, g] = kbuf[part[g], :].astype(F32).T
            keep(ODD, g, within(ODD, g, (zeros,) * TILES))

        @pl.when(later)
        def _():
            for which in range(2):
                for g in range(GROUPS):
                    raw_copy(which, g).start()

        for g in range(GROUPS):
            back_copy(g).wait_recv()
            lay(EVEN, g, past[g])
            ends(ODD, g, across(EVEN, g, kept(ODD, g)), True)
            respond(g)
        for g in range(GROUPS):
            z_copy(g).wait_recv()
            finish(g, zbuf, 1)
        for which in range(2):
            for g in range(GROUPS):
                raw_copy(which, g).wait_send()


def local(streams, medium_taps, decay_rates, mode_weights, skip_gain):
    channels = streams.shape[1]
    hbm = pl.BlockSpec(memory_space=pltpu.MemorySpace.HBM)
    vmem = pltpu.VMEM
    dma = pltpu.SemaphoreType.DMA
    return pl.pallas_call(
        kernel,
        out_shape=pltpu.VMEM((channels, CHUNK), BF16),
        in_specs=[hbm] * 5,
        out_specs=pl.BlockSpec(memory_space=pltpu.VMEM),
        scratch_shapes=[
            vmem((channels, CHUNK), BF16),
            vmem((channels, CHUNK), BF16),
            vmem((channels, CHUNK), BF16),
            vmem((channels, TAPS), F32),
            vmem((MODES, channels), F32),
            vmem((MODES, channels), F32),
            vmem((GROUPS, LANES), F32),
            vmem((2, GROUPS, LANES, CHUNK), BF16),
            vmem((GROUPS, LANES, CHUNK), BF16),
            vmem((3, GROUPS, CHUNK + 2 * SUBS, LANES), F32),
            vmem((2, GROUPS, CHUNK, LANES), F32),
            vmem((2, GROUPS, TILES, SUBS, LANES), F32),
            vmem((2, GROUPS, CHUNK, LANES), F32),
            vmem((GROUPS, MODES, 4, SUBS, LANES), F32),
            vmem((GROUPS, 6, MODES, LANES), F32),
            vmem((GROUPS, STEP, SUBS, LANES), F32),
            vmem((GROUPS, STEP, SUBS, LANES), F32),
            vmem((GROUPS, MODES, SUBS, LANES), F32),
            vmem((GROUPS, CHUNK, LANES), F32),
            vmem((2, GROUPS, MODES, LANES), F32),
            vmem((GROUPS, Y, MODES, LANES), F32),
            vmem((GROUPS, X, MODES, LANES), F32),
            vmem((GROUPS, 2, MODES, LANES), F32),
            dma((7,)),
            dma((2, GROUPS)),
            dma((2, GROUPS)),
            dma((GROUPS,)),
            dma((GROUPS,)),
            dma((GROUPS,)),
            dma((GROUPS, Y - 1)),
            dma((GROUPS, Y - 1)),
            dma((GROUPS, X - 1)),
            dma((GROUPS, X - 1)),
            dma((GROUPS,)),
            dma((GROUPS,)),
        ],
        name="gated_modal",
        compiler_params=pltpu.CompilerParams(collective_id=0, has_side_effects=True),
    )(
        streams,
        medium_taps,
        decay_rates.T,
        mode_weights.T,
        skip_gain.reshape(GROUPS, LANES),
    )


def solution(mesh):
    placed = (P(None, "tp", "ctx"), P("tp", None), P("tp", None), P("tp", None), P("tp"))
    return jax.shard_map(
        local, mesh=mesh, in_specs=placed, out_specs=P("tp", "ctx"), check_vma=False
    )
```

```python
import jax
import jax.numpy as jnp
from jax import lax
from jax.experimental import pallas as pl
from jax.experimental.pallas import tpu as pltpu
from jax.sharding import PartitionSpec as P

MESH = pl.DeviceIdType.MESH
F32 = jnp.float32
BF16 = jnp.bfloat16
PAIRS = 32
LANES = 128
CHUNK = 128
TAPS = 128
MODES = 16
SUBS = 8
STEP = CHUNK // SUBS
TILES = CHUNK // SUBS
GROUPS = 2
EVEN, ODD, PAST = 0, 1, 2


def remote(src, dst, send, recv, ctx):
    return pltpu.make_async_remote_copy(
        src_ref=src,
        dst_ref=dst,
        send_sem=send,
        recv_sem=recv,
        device_id=(ctx, lax.axis_index("tp")),
        device_id_type=MESH,
    )


def wide(row):
    return jnp.broadcast_to(row, (SUBS, LANES))


def kernel(
    streams, taps, rates, weights, skip, out,
    vbuf, kbuf, qbuf, traw, rates_t, weights_t, direct,
    raw, past, tokens, keys, medium, series, coef, rows, gated, local, carry, mixed,
    state, sums, zbuf,
    in_sem, raw_send, raw_sem, past_send, past_sem, back_send,
    sum_send, sum_sem, z_send, z_sem,
):
    ctx = lax.axis_index("ctx")
    tp = lax.axis_index("tp")
    pair, hi = ctx // 2, ctx % 2
    low = tp // 2
    mate = ctx + 1 - 2 * hi
    after = PAIRS - 1 - pair
    soon = jnp.logical_and(low != 3, jnp.logical_and(low != 5, low != 7))
    late = jnp.logical_or(low == 5, low == 7)
    barrier = pltpu.get_barrier_semaphore()
    part = [pl.ds(g * LANES, LANES) for g in range(GROUPS)]

    def raw_copy(which, g):
        return remote(
            streams.at[2 - which, part[g], :], raw.at[which, g],
            raw_send.at[which, g], raw_sem.at[which, g], mate,
        )

    def forward_copy(g):
        return remote(raw.at[0, g], past.at[g], past_send.at[g], past_sem.at[g], ctx + 2)

    def back_copy(g):
        return remote(streams.at[2, part[g], :], past.at[g], back_send.at[g], past_sem.at[g], mate)

    def pair_copy(n):
        return remote(sums.at[0], sums.at[n], sum_send.at[n], sum_sem.at[n], ctx + 2 * n)

    def start_raw():
        for which in range(2):
            for g in range(GROUPS):
                raw_copy(which, g).start()

    def z_copy(g):
        return remote(zbuf.at[g, 0], zbuf.at[g, 1], z_send.at[g], z_sem.at[g], mate)

    @pl.when(hi == 0)
    def _():
        pl.semaphore_signal(barrier, inc=1, device_id=(mate, tp), device_id_type=MESH)

        @pl.loop(1, pair + 1)
        def _(n):
            pl.semaphore_signal(
                barrier, inc=1, device_id=(ctx - 2 * n, tp), device_id_type=MESH
            )

    @pl.when(hi == 1)
    def _():
        pl.semaphore_wait(barrier, 1)

        @pl.when(soon)
        def _():
            start_raw()

    loads = []
    for n, (src, dst) in enumerate(
        ((rates, rates_t), (weights, weights_t), (taps, traw), (streams.at[2], vbuf),
         (streams.at[1], kbuf), (skip, direct), (streams.at[0], qbuf))
    ):
        copy = pltpu.make_async_copy(src, dst, in_sem.at[n])
        copy.start()
        loads.append(copy)

    sub = lax.broadcasted_iota(jnp.int32, (SUBS, LANES), 0)
    subf = sub.astype(F32)
    loads[0].wait()
    loads[1].wait()
    for g in range(GROUPS):
        rate = rates_t[:, part[g]]
        rows[g, 0] = jnp.exp(-rate)
        rows[g, 1] = weights_t[:, part[g]] * jnp.sqrt(2.0 * rate)
        rows[g, 2] = jnp.exp(-128.0 * rate)
        rows[g, 3] = jnp.exp(-256.0 * rate)
        for r in range(MODES):
            lam = wide(rates_t[r : r + 1, part[g]])
            coef[g, r, 0] = jnp.where(sub >= 1, jnp.exp(-16.0 * lam), 0.0)
            coef[g, r, 1] = jnp.where(sub >= 2, jnp.exp(-32.0 * lam), 0.0)
            coef[g, r, 2] = jnp.where(sub >= 4, jnp.exp(-64.0 * lam), 0.0)
            coef[g, r, 3] = jnp.exp(-16.0 * subf * lam)

    @pl.when(jnp.logical_and(hi == 1, low == 3))
    def _():
        start_raw()

    for n in range(2, 7):
        loads[n].wait()
    zeros = jnp.zeros((SUBS, LANES), F32)

    def lay(which, g, block):
        tokens[which, g, pl.ds(0, SUBS), :] = zeros
        tokens[which, g, pl.ds(SUBS, CHUNK), :] = block.astype(F32).T
        tokens[which, g, pl.ds(SUBS + CHUNK, SUBS), :] = zeros

    for g in range(GROUPS):
        traw[part[g], :] = traw[part[g], :].T

    def within(which, g, acc):
        def body(b, acc):
            acc = list(acc)
            window = [
                tokens[which, g, pl.ds(SUBS + SUBS * q - b, SUBS), :] for q in range(TILES)
            ]
            for a in range(TILES):
                tap = wide(traw[pl.ds(g * TAPS + SUBS * a + b, 1), :])
                for p in range(a, TILES):
                    acc[p] = acc[p] + tap * window[p - a]
            return tuple(acc)

        return lax.fori_loop(0, SUBS, body, tuple(acc))

    def across(which, g, acc):
        def body(b, acc):
            acc = list(acc)
            window = [
                tokens[which, g, pl.ds(2 * SUBS + SUBS * q - b, SUBS), :] for q in range(TILES)
            ]
            for a in range(TILES):
                tap = wide(traw[pl.ds(g * TAPS + SUBS * a + b, 1), :])
                for p in range(a + 1):
                    acc[p] = acc[p] + tap * window[TILES - 1 + p - a]
            return tuple(acc)

        return lax.fori_loop(0, SUBS, body, tuple(acc))

    def keep(which, g, acc):
        for p in range(TILES):
            medium[which, g, p] = acc[p]

    def kept(which, g):
        return tuple(medium[which, g, p] for p in range(TILES))

    def ends(which, g, acc, mine):
        for p in range(TILES):
            key = keys[which, g, pl.ds(SUBS * p, SUBS), :]
            series[which, g, pl.ds(SUBS * p, SUBS), :] = (key * acc[p]).astype(BF16).astype(F32)
        gate = [series[which, g, pl.ds(i, SUBS, stride=STEP), :] for i in range(STEP)]
        if mine:
            for i in range(STEP):
                gated[g, i] = gate[i]
        for r in range(MODES):
            a = wide(rows[g, 0, r : r + 1, :])
            h = gate[0]
            for i in range(1, STEP):
                h = h * a + gate[i]
            h = h + coef[g, r, 0] * pltpu.roll(h, 1, 0)
            h = h + coef[g, r, 1] * pltpu.roll(h, 2, 0)
            h = h + coef[g, r, 2] * pltpu.roll(h, 4, 0)
            if mine:
                carry[g, r] = jnp.where(sub >= 1, pltpu.roll(h, 1, 0), 0.0)
            state[which, g, pl.ds(r, 1), :] = h[SUBS - 1 : SUBS, :]

    def respond(g):
        skipped = wide(direct[g : g + 1, :])
        start = tuple(skipped * gated[g, i] for i in range(STEP))

        def modes(block, acc):
            acc = list(acc)
            for rr in range(4):
                r = 4 * block + rr
                a = wide(rows[g, 0, pl.ds(r, 1), :])
                w = wide(rows[g, 1, pl.ds(r, 1), :])
                h = a * carry[g, r] + gated[g, 0]
                acc[0] = acc[0] + w * h
                for i in range(1, STEP):
                    h = h * a + gated[g, i]
                    acc[i] = acc[i] + w * h
            return tuple(acc)

        total = lax.fori_loop(0, MODES // 4, modes, start)
        for i in range(STEP):
            local[g, i] = total[i]

    def finish(g, held, n):
        acc = [local[g, i] for i in range(STEP)]
        for r in range(MODES):
            a = wide(rows[g, 0, r : r + 1, :])
            w = wide(rows[g, 1, r : r + 1, :])
            q = (w * a) * (coef[g, r, 3] * wide(held[g, n, r : r + 1, :]))
            acc[0] = acc[0] + q
            for i in range(1, STEP):
                q = q * a
                acc[i] = acc[i] + q
        for i in range(STEP):
            mixed[g, pl.ds(i, SUBS, stride=STEP), :] = acc[i]
        back = mixed[g].T.astype(BF16).astype(F32)
        out[part[g], :] = (qbuf[part[g], :].astype(F32) * back).astype(BF16)

    @pl.when(hi == 0)
    def _():
        for g in range(GROUPS):
            lay(EVEN, g, vbuf[part[g], :])
            keys[EVEN, g] = kbuf[part[g], :].astype(F32).T
            keep(EVEN, g, within(EVEN, g, (zeros,) * TILES))
            keep(ODD, g, across(EVEN, g, (zeros,) * TILES))

        @pl.when(after > 0)
        def _():
            pl.semaphore_wait(barrier, after)

        for g in range(GROUPS):
            raw_copy(0, g).wait_recv()

            @pl.when(after > 0)
            def _():
                forward_copy(g).start()

        for g in range(GROUPS):
            back_copy(g).start()
        for g in range(GROUPS):
            lay(ODD, g, raw[0, g])
            keep(ODD, g, within(ODD, g, kept(ODD, g)))
        for g in range(GROUPS):

            @pl.when(pair > 0)
            def _():
                forward_copy(g).wait_recv()

            @pl.when(pair == 0)
            def _():
                past[g] = jnp.zeros((LANES, CHUNK), BF16)

            lay(PAST, g, past[g])
            ends(EVEN, g, across(PAST, g, kept(EVEN, g)), True)
        for g in range(GROUPS):
            raw_copy(1, g).wait_recv()
            keys[ODD, g] = raw[1, g].astype(F32).T
            ends(ODD, g, kept(ODD, g), False)
            sums[0, g] = (rows[g, 2] * state[EVEN, g] + state[ODD, g]).astype(BF16)

        @pl.loop(1, after + 1)
        def _(n):
            pair_copy(n).start()

        for g in range(GROUPS):
            respond(g)

        @pl.loop(1, pair + 1)
        def _(n):
            pair_copy(n).wait_recv()

        def older(k, acc):
            term = sums[pair - k]
            return tuple(acc[g] * rows[g, 3] + term[g].astype(F32) for g in range(GROUPS))

        nothing = jnp.zeros((MODES, LANES), F32)
        planes = lax.fori_loop(0, pair, older, (nothing,) * GROUPS)
        for g in range(GROUPS):
            zbuf[g, 1] = planes[g]
            zbuf[g, 0] = rows[g, 2] * planes[g] + state[EVEN, g]
            z_copy(g).start()
        for g in range(GROUPS):
            finish(g, zbuf, 1)
        for g in range(GROUPS):

            @pl.when(after > 0)
            def _():
                forward_copy(g).wait_send()

            back_copy(g).wait_send()
            z_copy(g).wait_send()

        @pl.loop(1, after + 1)
        def _(n):
            pair_copy(n).wait_send()

    @pl.when(hi == 1)
    def _():
        for g in range(GROUPS):
            lay(ODD, g, vbuf[part[g], :])
            keys[ODD, g] = kbuf[part[g], :].astype(F32).T
            keep(ODD, g, within(ODD, g, (zeros,) * TILES))

        @pl.when(late)
        def _():
            start_raw()

        for g in range(GROUPS):
            back_copy(g).wait_recv()
            lay(EVEN, g, past[g])
            ends(ODD, g, across(EVEN, g, kept(ODD, g)), True)
            respond(g)
        for g in range(GROUPS):
            z_copy(g).wait_recv()
            finish(g, zbuf, 1)
        for which in range(2):
            for g in range(GROUPS):
                raw_copy(which, g).wait_send()


def local(streams, medium_taps, decay_rates, mode_weights, skip_gain):
    channels = streams.shape[1]
    hbm = pl.BlockSpec(memory_space=pltpu.MemorySpace.HBM)
    vmem = pltpu.VMEM
    dma = pltpu.SemaphoreType.DMA
    return pl.pallas_call(
        kernel,
        out_shape=pltpu.VMEM((channels, CHUNK), BF16),
        in_specs=[hbm] * 5,
        out_specs=pl.BlockSpec(memory_space=pltpu.VMEM),
        scratch_shapes=[
            vmem((channels, CHUNK), BF16),
            vmem((channels, CHUNK), BF16),
            vmem((channels, CHUNK), BF16),
            vmem((channels, TAPS), F32),
            vmem((MODES, channels), F32),
            vmem((MODES, channels), F32),
            vmem((GROUPS, LANES), F32),
            vmem((2, GROUPS, LANES, CHUNK), BF16),
            vmem((GROUPS, LANES, CHUNK), BF16),
            vmem((3, GROUPS, CHUNK + 2 * SUBS, LANES), F32),
            vmem((2, GROUPS, CHUNK, LANES), F32),
            vmem((2, GROUPS, TILES, SUBS, LANES), F32),
            vmem((2, GROUPS, CHUNK, LANES), F32),
            vmem((GROUPS, MODES, 4, SUBS, LANES), F32),
            vmem((GROUPS, 4, MODES, LANES), F32),
            vmem((GROUPS, STEP, SUBS, LANES), F32),
            vmem((GROUPS, STEP, SUBS, LANES), F32),
            vmem((GROUPS, MODES, SUBS, LANES), F32),
            vmem((GROUPS, CHUNK, LANES), F32),
            vmem((2, GROUPS, MODES, LANES), F32),
            vmem((PAIRS, GROUPS, MODES, LANES), BF16),
            vmem((GROUPS, 2, MODES, LANES), F32),
            dma((7,)),
            dma((2, GROUPS)),
            dma((2, GROUPS)),
            dma((GROUPS,)),
            dma((GROUPS,)),
            dma((GROUPS,)),
            dma((PAIRS,)),
            dma((PAIRS,)),
            dma((GROUPS,)),
            dma((GROUPS,)),
        ],
        name="gated_modal",
        compiler_params=pltpu.CompilerParams(collective_id=0, has_side_effects=True),
    )(
        streams,
        medium_taps,
        decay_rates.T,
        mode_weights.T,
        skip_gain.reshape(GROUPS, LANES),
    )


def solution(mesh):
    placed = (P(None, "tp", "ctx"), P("tp", None), P("tp", None), P("tp", None), P("tp"))
    return jax.shard_map(
        local, mesh=mesh, in_specs=placed, out_specs=P("tp", "ctx"), check_vma=False
    )
```

```python
import jax
import jax.numpy as jnp
from jax import lax
from jax.experimental import pallas as pl
from jax.experimental.pallas import tpu as pltpu
from jax.sharding import PartitionSpec as P

MESH = pl.DeviceIdType.MESH
F32 = jnp.float32
BF16 = jnp.bfloat16
PAIRS = 32
ROWS = 4
LANES = 128
CHUNK = 128
TAPS = 128
MODES = 16
SUBS = 8
STEP = CHUNK // SUBS
TILES = CHUNK // SUBS
GROUPS = 2
EVEN, ODD, PAST = 0, 1, 2


def remote(src, dst, send, recv, ctx):
    return pltpu.make_async_remote_copy(
        src_ref=src,
        dst_ref=dst,
        send_sem=send,
        recv_sem=recv,
        device_id=(ctx, lax.axis_index("tp")),
        device_id_type=MESH,
    )


def wide(row):
    return jnp.broadcast_to(row, (SUBS, LANES))


def kernel(
    streams, taps, rates, weights, skip, out,
    vbuf, kbuf, qbuf, traw, rates_t, weights_t, direct,
    raw, past, tokens, keys, medium, series, coef, rows, gated, local, carry, mixed,
    state, sums, zbuf,
    in_sem, raw_send, raw_sem, past_send, past_sem, back_send,
    sum_send, sum_sem, z_send, z_sem,
):
    ctx = lax.axis_index("ctx")
    tp = lax.axis_index("tp")
    pair, hi = ctx // 2, ctx % 2
    low = tp // 2
    mate = ctx + 1 - 2 * hi
    after = PAIRS - 1 - pair
    soon = jnp.logical_and(low != 3, jnp.logical_and(low != 5, low != 7))
    late = jnp.logical_or(low == 5, low == 7)
    barrier = pltpu.get_barrier_semaphore()
    part = [pl.ds(g * LANES, LANES) for g in range(GROUPS)]

    def raw_copy(which, g):
        return remote(
            streams.at[2 - which, part[g], :], raw.at[which, g],
            raw_send.at[which, g], raw_sem.at[which, g], mate,
        )

    def forward_copy(g):
        return remote(raw.at[0, g], past.at[g], past_send.at[g], past_sem.at[g], ctx + 2)

    def back_copy(g):
        return remote(streams.at[2, part[g], :], past.at[g], back_send.at[g], past_sem.at[g], mate)

    def pair_copy(n):
        return remote(sums.at[0], sums.at[n], sum_send.at[n], sum_sem.at[n], ctx + 2 * n)

    def start_raw():
        for which in range(2):
            for g in range(GROUPS):
                raw_copy(which, g).start()

    def z_copy():
        return remote(zbuf.at[0], zbuf.at[1], z_send, z_sem, mate)

    @pl.when(hi == 0)
    def _():
        pl.semaphore_signal(barrier, inc=1, device_id=(mate, tp), device_id_type=MESH)

        @pl.loop(1, pair + 1)
        def _(n):
            pl.semaphore_signal(
                barrier, inc=1, device_id=(ctx - 2 * n, tp), device_id_type=MESH
            )

    @pl.when(hi == 1)
    def _():
        pl.semaphore_wait(barrier, 1)

        @pl.when(soon)
        def _():
            start_raw()

    loads = []
    for n, (src, dst) in enumerate(
        ((rates, rates_t), (weights, weights_t), (taps, traw), (streams.at[2], vbuf),
         (streams.at[1], kbuf), (skip, direct), (streams.at[0], qbuf))
    ):
        copy = pltpu.make_async_copy(src, dst, in_sem.at[n])
        copy.start()
        loads.append(copy)

    sub = lax.broadcasted_iota(jnp.int32, (SUBS, LANES), 0)
    subf = sub.astype(F32)
    loads[0].wait()
    loads[1].wait()
    for g in range(GROUPS):
        rate = rates_t[:, part[g]]
        rows[g, 0] = jnp.exp(-rate)
        rows[g, 1] = weights_t[:, part[g]] * jnp.sqrt(2.0 * rate)
        rows[g, 2] = jnp.exp(-128.0 * rate)
        rows[g, 3] = jnp.exp(-256.0 * rate)
        for r in range(MODES):
            lam = wide(rates_t[r : r + 1, part[g]])
            coef[g, r, 0] = jnp.where(sub >= 1, jnp.exp(-16.0 * lam), 0.0)
            coef[g, r, 1] = jnp.where(sub >= 2, jnp.exp(-32.0 * lam), 0.0)
            coef[g, r, 2] = jnp.where(sub >= 4, jnp.exp(-64.0 * lam), 0.0)
            coef[g, r, 3] = jnp.exp(-16.0 * subf * lam)

    @pl.when(jnp.logical_and(hi == 1, low == 3))
    def _():
        start_raw()

    for n in range(2, 7):
        loads[n].wait()
    zeros = jnp.zeros((SUBS, LANES), F32)

    def lay(which, g, block):
        tokens[which, g, pl.ds(0, SUBS), :] = zeros
        tokens[which, g, pl.ds(SUBS, CHUNK), :] = block.astype(F32).T
        tokens[which, g, pl.ds(SUBS + CHUNK, SUBS), :] = zeros

    for g in range(GROUPS):
        traw[part[g], :] = traw[part[g], :].T

    def within(which, g, acc):
        def body(b, acc):
            acc = list(acc)
            window = [
                tokens[which, g, pl.ds(SUBS + SUBS * q - b, SUBS), :] for q in range(TILES)
            ]
            for a in range(TILES):
                tap = wide(traw[pl.ds(g * TAPS + SUBS * a + b, 1), :])
                for p in range(a, TILES):
                    acc[p] = acc[p] + tap * window[p - a]
            return tuple(acc)

        return lax.fori_loop(0, SUBS, body, tuple(acc))

    def across(which, g, acc):
        def body(b, acc):
            acc = list(acc)
            window = [
                tokens[which, g, pl.ds(2 * SUBS + SUBS * q - b, SUBS), :] for q in range(TILES)
            ]
            for a in range(TILES):
                tap = wide(traw[pl.ds(g * TAPS + SUBS * a + b, 1), :])
                for p in range(a + 1):
                    acc[p] = acc[p] + tap * window[TILES - 1 + p - a]
            return tuple(acc)

        return lax.fori_loop(0, SUBS, body, tuple(acc))

    def keep(which, g, acc):
        for p in range(TILES):
            medium[which, g, p] = acc[p]

    def kept(which, g):
        return tuple(medium[which, g, p] for p in range(TILES))

    def ends(which, g, acc, mine):
        for p in range(TILES):
            key = keys[which, g, pl.ds(SUBS * p, SUBS), :]
            series[which, g, pl.ds(SUBS * p, SUBS), :] = (key * acc[p]).astype(BF16).astype(F32)
        gate = [series[which, g, pl.ds(i, SUBS, stride=STEP), :] for i in range(STEP)]
        if mine:
            for i in range(STEP):
                gated[g, i] = gate[i]
        for r in range(MODES):
            a = wide(rows[g, 0, r : r + 1, :])
            h = gate[0]
            for i in range(1, STEP):
                h = h * a + gate[i]
            h = h + coef[g, r, 0] * pltpu.roll(h, 1, 0)
            h = h + coef[g, r, 1] * pltpu.roll(h, 2, 0)
            h = h + coef[g, r, 2] * pltpu.roll(h, 4, 0)
            if mine:
                carry[g, r] = jnp.where(sub >= 1, pltpu.roll(h, 1, 0), 0.0)
            state[which, g, pl.ds(r, 1), :] = h[SUBS - 1 : SUBS, :]

    def respond(g):
        skipped = wide(direct[g : g + 1, :])
        start = tuple(skipped * gated[g, i] for i in range(STEP))

        def modes(block, acc):
            acc = list(acc)
            for rr in range(4):
                r = 4 * block + rr
                a = wide(rows[g, 0, pl.ds(r, 1), :])
                w = wide(rows[g, 1, pl.ds(r, 1), :])
                h = a * carry[g, r] + gated[g, 0]
                acc[0] = acc[0] + w * h
                for i in range(1, STEP):
                    h = h * a + gated[g, i]
                    acc[i] = acc[i] + w * h
            return tuple(acc)

        total = lax.fori_loop(0, MODES // 4, modes, start)
        for i in range(STEP):
            local[g, i] = total[i]

    def finish(g, held):
        acc = [local[g, i] for i in range(STEP)]
        for r in range(MODES):
            a = wide(rows[g, 0, r : r + 1, :])
            w = wide(rows[g, 1, r : r + 1, :])
            q = (w * a) * (coef[g, r, 3] * wide(held[g, r : r + 1, :]))
            acc[0] = acc[0] + q
            for i in range(1, STEP):
                q = q * a
                acc[i] = acc[i] + q
        for i in range(STEP):
            mixed[g, pl.ds(i, SUBS, stride=STEP), :] = acc[i]
        back = mixed[g].T.astype(BF16).astype(F32)
        out[part[g], :] = (qbuf[part[g], :].astype(F32) * back).astype(BF16)

    @pl.when(hi == 0)
    def _():
        for g in range(GROUPS):
            lay(EVEN, g, vbuf[part[g], :])
            keys[EVEN, g] = kbuf[part[g], :].astype(F32).T
            keep(EVEN, g, within(EVEN, g, (zeros,) * TILES))
            keep(ODD, g, across(EVEN, g, (zeros,) * TILES))

        @pl.when(after > 0)
        def _():
            pl.semaphore_wait(barrier, after)

        for g in range(GROUPS):
            raw_copy(0, g).wait_recv()

            @pl.when(after > 0)
            def _():
                forward_copy(g).start()

        for g in range(GROUPS):
            back_copy(g).start()
        for g in range(GROUPS):
            lay(ODD, g, raw[0, g])
            keep(ODD, g, within(ODD, g, kept(ODD, g)))
        for g in range(GROUPS):

            @pl.when(pair > 0)
            def _():
                forward_copy(g).wait_recv()

            @pl.when(pair == 0)
            def _():
                past[g] = jnp.zeros((LANES, CHUNK), BF16)

            lay(PAST, g, past[g])
            ends(EVEN, g, across(PAST, g, kept(EVEN, g)), True)
        for g in range(GROUPS):
            raw_copy(1, g).wait_recv()
            keys[ODD, g] = raw[1, g].astype(F32).T
            ends(ODD, g, kept(ODD, g), False)
            sums[0, g] = (rows[g, 2] * state[EVEN, g] + state[ODD, g]).astype(BF16)

        @pl.loop(0, PAIRS)
        def _(m):
            target = lax.rem(m, ROWS) * (PAIRS // ROWS) + m // ROWS

            @pl.when(target > pair)
            def _():
                pair_copy(target - pair).start()

        for g in range(GROUPS):
            respond(g)

        @pl.loop(1, pair + 1)
        def _(n):
            pair_copy(n).wait_recv()

        def older(k, acc):
            term = sums[pair - k]
            return tuple(acc[g] * rows[g, 3] + term[g].astype(F32) for g in range(GROUPS))

        nothing = jnp.zeros((MODES, LANES), F32)
        planes = lax.fori_loop(0, pair, older, (nothing,) * GROUPS)
        for g in range(GROUPS):
            zbuf[0, g] = rows[g, 2] * planes[g] + state[EVEN, g]
        z_copy().start()
        for g in range(GROUPS):
            zbuf[1, g] = planes[g]
        for g in range(GROUPS):
            finish(g, zbuf.at[1])
        for g in range(GROUPS):

            @pl.when(after > 0)
            def _():
                forward_copy(g).wait_send()

            back_copy(g).wait_send()

        @pl.loop(1, after + 1)
        def _(n):
            pair_copy(n).wait_send()

        z_copy().wait_send()

    @pl.when(hi == 1)
    def _():
        for g in range(GROUPS):
            lay(ODD, g, vbuf[part[g], :])
            keys[ODD, g] = kbuf[part[g], :].astype(F32).T
            keep(ODD, g, within(ODD, g, (zeros,) * TILES))

        @pl.when(late)
        def _():
            start_raw()

        for g in range(GROUPS):
            back_copy(g).wait_recv()
            lay(EVEN, g, past[g])
            ends(ODD, g, across(EVEN, g, kept(ODD, g)), True)
            respond(g)
        z_copy().wait_recv()
        for g in range(GROUPS):
            finish(g, zbuf.at[1])
        for which in range(2):
            for g in range(GROUPS):
                raw_copy(which, g).wait_send()


def local(streams, medium_taps, decay_rates, mode_weights, skip_gain):
    channels = streams.shape[1]
    hbm = pl.BlockSpec(memory_space=pltpu.MemorySpace.HBM)
    vmem = pltpu.VMEM
    dma = pltpu.SemaphoreType.DMA
    return pl.pallas_call(
        kernel,
        out_shape=pltpu.VMEM((channels, CHUNK), BF16),
        in_specs=[hbm] * 5,
        out_specs=pl.BlockSpec(memory_space=pltpu.VMEM),
        scratch_shapes=[
            vmem((channels, CHUNK), BF16),
            vmem((channels, CHUNK), BF16),
            vmem((channels, CHUNK), BF16),
            vmem((channels, TAPS), F32),
            vmem((MODES, channels), F32),
            vmem((MODES, channels), F32),
            vmem((GROUPS, LANES), F32),
            vmem((2, GROUPS, LANES, CHUNK), BF16),
            vmem((GROUPS, LANES, CHUNK), BF16),
            vmem((3, GROUPS, CHUNK + 2 * SUBS, LANES), F32),
            vmem((2, GROUPS, CHUNK, LANES), F32),
            vmem((2, GROUPS, TILES, SUBS, LANES), F32),
            vmem((2, GROUPS, CHUNK, LANES), F32),
            vmem((GROUPS, MODES, 4, SUBS, LANES), F32),
            vmem((GROUPS, 4, MODES, LANES), F32),
            vmem((GROUPS, STEP, SUBS, LANES), F32),
            vmem((GROUPS, STEP, SUBS, LANES), F32),
            vmem((GROUPS, MODES, SUBS, LANES), F32),
            vmem((GROUPS, CHUNK, LANES), F32),
            vmem((2, GROUPS, MODES, LANES), F32),
            vmem((PAIRS, GROUPS, MODES, LANES), BF16),
            vmem((2, GROUPS, MODES, LANES), F32),
            dma((7,)),
            dma((2, GROUPS)),
            dma((2, GROUPS)),
            dma((GROUPS,)),
            dma((GROUPS,)),
            dma((GROUPS,)),
            dma((PAIRS,)),
            dma((PAIRS,)),
            pltpu.SemaphoreType.DMA,
            pltpu.SemaphoreType.DMA,
        ],
        name="gated_modal",
        compiler_params=pltpu.CompilerParams(collective_id=0, has_side_effects=True),
    )(
        streams,
        medium_taps,
        decay_rates.T,
        mode_weights.T,
        skip_gain.reshape(GROUPS, LANES),
    )


def solution(mesh):
    placed = (P(None, "tp", "ctx"), P("tp", None), P("tp", None), P("tp", None), P("tp"))
    return jax.shard_map(
        local, mesh=mesh, in_specs=placed, out_specs=P("tp", "ctx"), check_vma=False
    )
```

```python
import jax
import jax.numpy as jnp
from jax import lax
from jax.experimental import pallas as pl
from jax.experimental.pallas import tpu as pltpu
from jax.sharding import PartitionSpec as P

MESH = pl.DeviceIdType.MESH
F32 = jnp.float32
BF16 = jnp.bfloat16
PAIRS = 32
ROWS = 4
LANES = 128
CHUNK = 128
TAPS = 128
MODES = 16
SUBS = 8
STEP = CHUNK // SUBS
TILES = CHUNK // SUBS
GROUPS = 2
EVEN, ODD, PAST = 0, 1, 2


def remote(src, dst, send, recv, ctx):
    return pltpu.make_async_remote_copy(
        src_ref=src,
        dst_ref=dst,
        send_sem=send,
        recv_sem=recv,
        device_id=(ctx, lax.axis_index("tp")),
        device_id_type=MESH,
    )


def wide(row):
    return jnp.broadcast_to(row, (SUBS, LANES))


def kernel(
    streams, taps, rates, weights, skip, out,
    vbuf, kbuf, qbuf, traw, rates_t, weights_t, direct,
    raw, past, tokens, keys, medium, series, coef, rows, gated, local, carry, mixed,
    state, sums, zbuf,
    in_sem, raw_send, raw_sem, past_send, past_sem, back_send,
    sum_send, sum_sem, z_send, z_sem,
):
    ctx = lax.axis_index("ctx")
    tp = lax.axis_index("tp")
    pair, hi = ctx // 2, ctx % 2
    low = tp // 2
    mate = ctx + 1 - 2 * hi
    after = PAIRS - 1 - pair
    soon = jnp.logical_and(low != 3, jnp.logical_and(low != 5, low != 7))
    late = jnp.logical_or(low == 5, low == 7)
    barrier = pltpu.get_barrier_semaphore()
    part = [pl.ds(g * LANES, LANES) for g in range(GROUPS)]

    def raw_copy(which, g):
        return remote(
            streams.at[2 - which, part[g], :], raw.at[which, g],
            raw_send.at[which, g], raw_sem.at[which, g], mate,
        )

    def forward_copy(g):
        return remote(raw.at[0, g], past.at[g], past_send.at[g], past_sem.at[g], ctx + 2)

    def back_copy(g):
        return remote(streams.at[2, part[g], :], past.at[g], back_send.at[g], past_sem.at[g], mate)

    def pair_copy(n):
        return remote(sums.at[0], sums.at[n], sum_send.at[n], sum_sem.at[n], ctx + 2 * n)

    def start_raw():
        for which in range(2):
            for g in range(GROUPS):
                raw_copy(which, g).start()

    def z_copy():
        return remote(zbuf.at[0], zbuf.at[1], z_send, z_sem, mate)

    @pl.when(hi == 0)
    def _():
        pl.semaphore_signal(barrier, inc=1, device_id=(mate, tp), device_id_type=MESH)

        @pl.loop(1, pair + 1)
        def _(n):
            pl.semaphore_signal(
                barrier, inc=1, device_id=(ctx - 2 * n, tp), device_id_type=MESH
            )

    @pl.when(hi == 1)
    def _():
        pl.semaphore_wait(barrier, 1)

        @pl.when(soon)
        def _():
            start_raw()

    loads = []
    for n, (src, dst) in enumerate(
        ((rates, rates_t), (weights, weights_t), (taps, traw), (streams.at[2], vbuf),
         (streams.at[1], kbuf), (skip, direct), (streams.at[0], qbuf))
    ):
        copy = pltpu.make_async_copy(src, dst, in_sem.at[n])
        copy.start()
        loads.append(copy)

    sub = lax.broadcasted_iota(jnp.int32, (SUBS, LANES), 0)
    subf = sub.astype(F32)
    loads[0].wait()
    loads[1].wait()
    for g in range(GROUPS):
        rate = rates_t[:, part[g]]
        rows[g, 0] = jnp.exp(-rate)
        rows[g, 1] = weights_t[:, part[g]] * jnp.sqrt(2.0 * rate)
        rows[g, 2] = jnp.exp(-128.0 * rate)
        rows[g, 3] = jnp.exp(-256.0 * rate)
        for r in range(MODES):
            lam = wide(rates_t[r : r + 1, part[g]])
            coef[g, r, 0] = jnp.where(sub >= 1, jnp.exp(-16.0 * lam), 0.0)
            coef[g, r, 1] = jnp.where(sub >= 2, jnp.exp(-32.0 * lam), 0.0)
            coef[g, r, 2] = jnp.where(sub >= 4, jnp.exp(-64.0 * lam), 0.0)
            coef[g, r, 3] = jnp.exp(-16.0 * subf * lam)

    @pl.when(jnp.logical_and(hi == 1, low == 3))
    def _():
        start_raw()

    for n in range(2, 7):
        loads[n].wait()
    zeros = jnp.zeros((SUBS, LANES), F32)

    def lay(which, g, block):
        tokens[which, g, pl.ds(0, SUBS), :] = zeros
        tokens[which, g, pl.ds(SUBS, CHUNK), :] = block.astype(F32).T
        tokens[which, g, pl.ds(SUBS + CHUNK, SUBS), :] = zeros

    for g in range(GROUPS):
        traw[part[g], :] = traw[part[g], :].T

    def within(which, g, acc):
        def body(b, acc):
            acc = list(acc)
            window = [
                tokens[which, g, pl.ds(SUBS + SUBS * q - b, SUBS), :] for q in range(TILES)
            ]
            for a in range(TILES):
                tap = wide(traw[pl.ds(g * TAPS + SUBS * a + b, 1), :])
                for p in range(a, TILES):
                    acc[p] = acc[p] + tap * window[p - a]
            return tuple(acc)

        return lax.fori_loop(0, SUBS, body, tuple(acc))

    def across(which, g, acc):
        def body(b, acc):
            acc = list(acc)
            window = [
                tokens[which, g, pl.ds(2 * SUBS + SUBS * q - b, SUBS), :] for q in range(TILES)
            ]
            for a in range(TILES):
                tap = wide(traw[pl.ds(g * TAPS + SUBS * a + b, 1), :])
                for p in range(a + 1):
                    acc[p] = acc[p] + tap * window[TILES - 1 + p - a]
            return tuple(acc)

        return lax.fori_loop(0, SUBS, body, tuple(acc))

    def keep(which, g, acc):
        for p in range(TILES):
            medium[which, g, p] = acc[p]

    def kept(which, g):
        return tuple(medium[which, g, p] for p in range(TILES))

    def ends(which, g, acc, mine):
        for p in range(TILES):
            key = keys[which, g, pl.ds(SUBS * p, SUBS), :]
            series[which, g, pl.ds(SUBS * p, SUBS), :] = (key * acc[p]).astype(BF16).astype(F32)
        gate = [series[which, g, pl.ds(i, SUBS, stride=STEP), :] for i in range(STEP)]
        if mine:
            for i in range(STEP):
                gated[g, i] = gate[i]
        for r in range(MODES):
            a = wide(rows[g, 0, r : r + 1, :])
            h = gate[0]
            for i in range(1, STEP):
                h = h * a + gate[i]
            h = h + coef[g, r, 0] * pltpu.roll(h, 1, 0)
            h = h + coef[g, r, 1] * pltpu.roll(h, 2, 0)
            h = h + coef[g, r, 2] * pltpu.roll(h, 4, 0)
            if mine:
                carry[g, r] = jnp.where(sub >= 1, pltpu.roll(h, 1, 0), 0.0)
            state[which, g, pl.ds(r, 1), :] = h[SUBS - 1 : SUBS, :]

    def respond(g):
        skipped = wide(direct[g : g + 1, :])
        start = tuple(skipped * gated[g, i] for i in range(STEP))

        def modes(block, acc):
            acc = list(acc)
            for rr in range(4):
                r = 4 * block + rr
                a = wide(rows[g, 0, pl.ds(r, 1), :])
                w = wide(rows[g, 1, pl.ds(r, 1), :])
                h = a * carry[g, r] + gated[g, 0]
                acc[0] = acc[0] + w * h
                for i in range(1, STEP):
                    h = h * a + gated[g, i]
                    acc[i] = acc[i] + w * h
            return tuple(acc)

        total = lax.fori_loop(0, MODES // 4, modes, start)
        for i in range(STEP):
            local[g, i] = total[i]

    def finish(g, held):
        acc = [local[g, i] for i in range(STEP)]
        for r in range(MODES):
            a = wide(rows[g, 0, r : r + 1, :])
            w = wide(rows[g, 1, r : r + 1, :])
            q = (w * a) * (coef[g, r, 3] * wide(held[g, r : r + 1, :]))
            acc[0] = acc[0] + q
            for i in range(1, STEP):
                q = q * a
                acc[i] = acc[i] + q
        for i in range(STEP):
            mixed[g, pl.ds(i, SUBS, stride=STEP), :] = acc[i]
        back = mixed[g].T.astype(BF16).astype(F32)
        out[part[g], :] = (qbuf[part[g], :].astype(F32) * back).astype(BF16)

    @pl.when(hi == 0)
    def _():
        for g in range(GROUPS):
            lay(EVEN, g, vbuf[part[g], :])
            keys[EVEN, g] = kbuf[part[g], :].astype(F32).T
            keep(EVEN, g, within(EVEN, g, (zeros,) * TILES))
            keep(ODD, g, across(EVEN, g, (zeros,) * TILES))

        @pl.when(after > 0)
        def _():
            pl.semaphore_wait(barrier, after)

        for g in range(GROUPS):
            raw_copy(0, g).wait_recv()

            @pl.when(after > 0)
            def _():
                forward_copy(g).start()

        for g in range(GROUPS):
            back_copy(g).start()
        for g in range(GROUPS):
            lay(ODD, g, raw[0, g])
            keep(ODD, g, within(ODD, g, kept(ODD, g)))
        for g in range(GROUPS):
            raw_copy(1, g).wait_recv()
            keys[ODD, g] = raw[1, g].astype(F32).T
            ends(ODD, g, kept(ODD, g), False)
        for g in range(GROUPS):

            @pl.when(pair > 0)
            def _():
                forward_copy(g).wait_recv()

            @pl.when(pair == 0)
            def _():
                past[g] = jnp.zeros((LANES, CHUNK), BF16)

            lay(PAST, g, past[g])
            ends(EVEN, g, across(PAST, g, kept(EVEN, g)), True)
            sums[0, g] = (rows[g, 2] * state[EVEN, g] + state[ODD, g]).astype(BF16)

        @pl.loop(0, PAIRS)
        def _(m):
            target = (ROWS - 1 - lax.rem(m, ROWS)) * (PAIRS // ROWS) + m // ROWS

            @pl.when(target > pair)
            def _():
                pair_copy(target - pair).start()

        for g in range(GROUPS):
            respond(g)

        @pl.loop(1, pair + 1)
        def _(n):
            pair_copy(n).wait_recv()

        def older(k, acc):
            term = sums[pair - k]
            return tuple(acc[g] * rows[g, 3] + term[g].astype(F32) for g in range(GROUPS))

        nothing = jnp.zeros((MODES, LANES), F32)
        planes = lax.fori_loop(0, pair, older, (nothing,) * GROUPS)
        for g in range(GROUPS):
            zbuf[0, g] = rows[g, 2] * planes[g] + state[EVEN, g]
        z_copy().start()
        for g in range(GROUPS):
            zbuf[1, g] = planes[g]
        for g in range(GROUPS):
            finish(g, zbuf.at[1])
        for g in range(GROUPS):

            @pl.when(after > 0)
            def _():
                forward_copy(g).wait_send()

            back_copy(g).wait_send()

        @pl.loop(1, after + 1)
        def _(n):
            pair_copy(n).wait_send()

        z_copy().wait_send()

    @pl.when(hi == 1)
    def _():
        for g in range(GROUPS):
            lay(ODD, g, vbuf[part[g], :])
            keys[ODD, g] = kbuf[part[g], :].astype(F32).T
            keep(ODD, g, within(ODD, g, (zeros,) * TILES))

        @pl.when(late)
        def _():
            start_raw()

        for g in range(GROUPS):
            back_copy(g).wait_recv()
            lay(EVEN, g, past[g])
            ends(ODD, g, across(EVEN, g, kept(ODD, g)), True)
            respond(g)
        z_copy().wait_recv()
        for g in range(GROUPS):
            finish(g, zbuf.at[1])
        for which in range(2):
            for g in range(GROUPS):
                raw_copy(which, g).wait_send()


def local(streams, medium_taps, decay_rates, mode_weights, skip_gain):
    channels = streams.shape[1]
    hbm = pl.BlockSpec(memory_space=pltpu.MemorySpace.HBM)
    vmem = pltpu.VMEM
    dma = pltpu.SemaphoreType.DMA
    return pl.pallas_call(
        kernel,
        out_shape=pltpu.VMEM((channels, CHUNK), BF16),
        in_specs=[hbm] * 5,
        out_specs=pl.BlockSpec(memory_space=pltpu.VMEM),
        scratch_shapes=[
            vmem((channels, CHUNK), BF16),
            vmem((channels, CHUNK), BF16),
            vmem((channels, CHUNK), BF16),
            vmem((channels, TAPS), F32),
            vmem((MODES, channels), F32),
            vmem((MODES, channels), F32),
            vmem((GROUPS, LANES), F32),
            vmem((2, GROUPS, LANES, CHUNK), BF16),
            vmem((GROUPS, LANES, CHUNK), BF16),
            vmem((3, GROUPS, CHUNK + 2 * SUBS, LANES), F32),
            vmem((2, GROUPS, CHUNK, LANES), F32),
            vmem((2, GROUPS, TILES, SUBS, LANES), F32),
            vmem((2, GROUPS, CHUNK, LANES), F32),
            vmem((GROUPS, MODES, 4, SUBS, LANES), F32),
            vmem((GROUPS, 4, MODES, LANES), F32),
            vmem((GROUPS, STEP, SUBS, LANES), F32),
            vmem((GROUPS, STEP, SUBS, LANES), F32),
            vmem((GROUPS, MODES, SUBS, LANES), F32),
            vmem((GROUPS, CHUNK, LANES), F32),
            vmem((2, GROUPS, MODES, LANES), F32),
            vmem((PAIRS, GROUPS, MODES, LANES), BF16),
            vmem((2, GROUPS, MODES, LANES), F32),
            dma((7,)),
            dma((2, GROUPS)),
            dma((2, GROUPS)),
            dma((GROUPS,)),
            dma((GROUPS,)),
            dma((GROUPS,)),
            dma((PAIRS,)),
            dma((PAIRS,)),
            pltpu.SemaphoreType.DMA,
            pltpu.SemaphoreType.DMA,
        ],
        name="gated_modal",
        compiler_params=pltpu.CompilerParams(collective_id=0, has_side_effects=True),
    )(
        streams,
        medium_taps,
        decay_rates.T,
        mode_weights.T,
        skip_gain.reshape(GROUPS, LANES),
    )


def solution(mesh):
    placed = (P(None, "tp", "ctx"), P("tp", None), P("tp", None), P("tp", None), P("tp"))
    return jax.shard_map(
        local, mesh=mesh, in_specs=placed, out_specs=P("tp", "ctx"), check_vma=False
    )
```
